256 devices in a mesh: pair: 32 (over z_lo, y, x), sector: 8 (over z_hi, core).
Axes of the slice: x: 4, y: 4, z: 8 (z_hi: 4, z_lo: 2; z = z_hi * 2 + z_lo), core: 2. Of those that a mesh axis runs over, the one named last changes fastest.
Arguments:
- wavefunction: float32 [8, 512, 512], P('sector', 'pair'), may hold values from -6 to 6
- preconditioner: float32 [8, 512, 512], P('sector', 'pair'), may hold values from 0.5 to 4
- left_ops: float32 [96, 8, 512, 512], P('pair', 'sector'), may hold values from -0.25 to 0.25
- right_ops: float32 [96, 8, 512, 512], P('pair', 'sector'), may hold values from -0.01953125 to 0.01953125
- charges: int32 [96], P('pair'), may hold values from 0 to 2
- coupling: int32 [8, 3], P('sector'), may hold values 0 or 1
Outputs:
- new_state: float32 [8, 512, 512], P('sector', 'pair')
- new_image: float32 [8, 512, 512], P('sector', 'pair')
- energies: float32 [2], replicated
The draws below stay inside these ranges and needn't reach their ends.
All inputs are finite; a program needn't handle non-finite values. No bound on the sum of `coupling` on one device may be relied on, other than what follows from the above.
Results may differ from the reference program's by a relative error of at most 0.0003.
Values sent between devices are 32-bit elements; how exact they have to be, the bound alone decides.
A program may use at most 64 MiB of HBM per device.

```python
import math
import jax
import jax.numpy as jnp
from jax import lax

M = 512
PAIRS = 96
SECTORS = 8


def place_ends(entries, rng, smallest, high):
    shape = entries.shape
    place = [jax.random.randint(jax.random.fold_in(rng, axis), (), 0, shape[axis]) for axis in range(len(shape))]
    entries = entries.at[tuple(place)].set(smallest)
    longest = shape.index(max(shape))
    place[longest] = (place[longest] + 1) % shape[longest]
    return entries.at[tuple(place)].set(high)


def shard_levels(rng, extent, shards, low, top_value):
    level = 1.0
    for axis_at, parts in shards:
        steps = jax.random.uniform(jax.random.fold_in(jax.random.fold_in(rng, 6), axis_at), (parts,), jnp.float32, low / len(shards), top_value / len(shards))
        level = level * jnp.repeat(jnp.exp(steps), extent[axis_at] // parts).reshape((-1,) + (1,) * (len(extent) - 1 - axis_at))
    return level


def noise(key, shape, scale, limit, split=(), kind=jnp.bfloat16):
    gain = shard_levels(key, shape, split, -0.22, 0.18) if split else 1.0
    values = jax.random.normal(key, shape, jnp.float32) * scale * gain
    return jnp.minimum(jnp.maximum(values, -limit), limit).astype(kind)


def setup_inputs(seed: int = 0) -> dict:
    keys = jax.random.split(jax.random.key(seed), 7)
    wavefunction = noise(keys[0], (SECTORS, M, M), 1.0, 6.0, ((0, 8), (1, 32)), jnp.float32)
    preconditioner = jnp.clip(jnp.exp(math.log(4.0) - 2.0794415 * jax.random.uniform(keys[1], (SECTORS, M, M), jnp.float32) ** shard_levels(keys[1], (SECTORS, M, M), ((0, 8), (1, 32)), -0.2, 0.2)), 0.5, 4.0)
    left_ops = noise(keys[2], (PAIRS, SECTORS, M, M), M ** -0.5, 0.25, ((0, 32), (1, 8)), jnp.float32)
    right_ops = noise(keys[3], (PAIRS, SECTORS, M, M), (2 * M * PAIRS) ** -0.5, 0.01953125, ((0, 32), (1, 8)), jnp.float32)
    charges = place_ends(jax.random.randint(keys[4], (PAIRS,), 0, 3), jax.random.fold_in(keys[4], 1), 0, 2).astype(jnp.int32)
    coupling = place_ends((jax.random.randint(keys[5], (SECTORS, 3), 0, 4) < 3).astype(jnp.int32), jax.random.fold_in(keys[5], 1), 0, 1)
    return {"wavefunction": wavefunction, "preconditioner": preconditioner, "left_ops": left_ops, "right_ops": right_ops, "charges": charges, "coupling": coupling}


highest = lax.Precision.HIGHEST

def product(first, second):
    return jnp.dot(first, second, precision=highest, preferred_element_type=jnp.float32)

def sigma_apply(vector, left_ops, right_ops, charges, coupling):
    sectors = vector.shape[0]

    def add_pair(result, pair_index):
        charge_slot = charges[pair_index].astype(jnp.int32)
        for sector in range(sectors):
            target = ((sector + charge_slot - 1) % sectors).astype(jnp.int32)
            allowed = coupling[sector, charge_slot].astype(jnp.float32)
            left_block = left_ops[pair_index, sector]
            right_block = right_ops[pair_index, sector]
            forward = product(product(left_block, vector[sector]), right_block.T)
            source_block = lax.dynamic_index_in_dim(vector, target, 0, keepdims=False)
            backward = product(product(left_block.T, source_block), right_block)
            result = result.at[sector].add(allowed * backward)
            current = lax.dynamic_index_in_dim(result, target, 0, keepdims=False)
            result = lax.dynamic_update_index_in_dim(result, current + allowed * forward, target, 0)
        return (result, None)
    result, unused = lax.scan(add_pair, jnp.zeros_like(vector), jnp.arange(charges.shape[0], dtype=jnp.int32))
    return result

def reference(wavefunction, preconditioner, left_ops, right_ops, charges, coupling):
    first_image = sigma_apply(wavefunction, left_ops, right_ops, charges, coupling)
    norm_sq = jnp.sum(wavefunction * wavefunction)
    correlation = jnp.sum(wavefunction * first_image)
    theta = correlation / norm_sq
    inverse = lax.rsqrt(norm_sq)
    vector = wavefunction * inverse
    image = first_image * inverse
    residual = image - theta * vector
    correction = residual / preconditioner
    along = jnp.sum(vector * correction)
    orthogonal = correction - along * vector
    length_sq = jnp.sum(orthogonal * orthogonal)
    basis = orthogonal * lax.rsqrt(length_sq + 1e-30)
    second_image = sigma_apply(basis, left_ops, right_ops, charges, coupling)
    corner = jnp.sum(basis * second_image)
    cross = jnp.sum(vector * second_image)
    half = (theta - corner) / 2.0
    lowest = (theta + corner) / 2.0 - jnp.sqrt(half * half + cross * cross)
    first_weight = corner - lowest
    second_weight = -cross
    size_norm = jnp.sqrt(first_weight * first_weight + second_weight * second_weight + 1e-30)
    scale = jnp.sqrt(jnp.float32(wavefunction.size))
    factor_one = scale * first_weight / size_norm
    factor_two = scale * second_weight / size_norm
    new_state = factor_one * vector + factor_two * basis
    new_image = factor_one * image + factor_two * second_image
    energies = jnp.stack([theta, lowest]).astype(jnp.float32)
    return (new_state, new_image, energies)
```

```python
import math

import jax
import jax.numpy as jnp
from jax import lax
from jax.experimental import pallas as pl
from jax.experimental.pallas import tpu as pltpu
from jax.sharding import Mesh
from jax.sharding import PartitionSpec as P

SECTOR = ("zh", "core")
PAIR = ("zl", "y", "x")
MESH = pl.DeviceIdType.MESH
F32 = jnp.float32
BF16 = jnp.bfloat16

M = 512
ROWS = 16
PAIRS = 3
OUTER, OWN, OTHER = 0, 1, 2
WAVES = 2
CW = M // WAVES
TILE = (8, 128)


def split(x):
    high = x.astype(BF16)
    return high, (x - high.astype(F32)).astype(BF16)


def total(x):
    return jnp.sum(jnp.sum(x, axis=0, keepdims=True), axis=1, keepdims=True)


def dot(a, b):
    return jnp.dot(a, b, preferred_element_type=F32)


def kernel(
    charges,
    coupling,
    w_in,
    pre_in,
    l_hbm,
    r_hbm,
    state_out,
    image_out,
    energy_out,
    raw,
    lcat,
    ltcat,
    rcat,
    rtcat,
    v,
    vcat,
    ycat,
    zcat,
    fbuf,
    tsum,
    otherbuf,
    bulk_half,
    bulk_full,
    tail_half,
    tail_full,
    zbuf,
    image,
    corrected,
    arbuf,
    load_sem,
    z_s,
    z_r,
    ring_s,
    ring_r,
    other_s,
    other_r,
    rz_s,
    rz_r,
    rring_s,
    rring_r,
    rother_s,
    rother_r,
    ar_s,
    ar_r,
):
    zl, y, x = (lax.axis_index(a) for a in PAIR)
    zh, core = (lax.axis_index(a) for a in SECTOR)
    far = lax.rem(zh + 2 * core + 3, 4)
    plane, line = y * 4 + x, zl * 8 + zh * 2 + core

    def plane_peer(d):
        peer = lax.rem(plane + d, 16)
        return {"y": peer // 4, "x": lax.rem(peer, 4)}

    def line_peer(d):
        peer = lax.rem(line + d, 16)
        return {"zl": peer // 8, "zh": lax.rem(peer // 2, 4), "core": lax.rem(peer, 2)}

    peers = (plane_peer, line_peer)
    places = (plane, line)

    def copy(src, dst, send, recv, device):
        return pltpu.make_async_remote_copy(
            src_ref=src,
            dst_ref=dst,
            send_sem=send,
            recv_sem=recv,
            device_id=device,
            device_id_type=MESH,
        )

    loads = []
    for p in range(PAIRS):
        loads.append(
            (
                pltpu.make_async_copy(l_hbm.at[p], raw.at[0, p], load_sem.at[0, p]),
                pltpu.make_async_copy(r_hbm.at[p], raw.at[1, p], load_sem.at[1, p]),
            )
        )
        for c in loads[-1]:
            c.start()

    barrier = pltpu.get_barrier_semaphore()

    @pl.loop(1, 16)
    def _(d):
        pl.semaphore_signal(barrier, inc=1, device_id=plane_peer(d), device_id_type=MESH)
        pl.semaphore_signal(barrier, inc=1, device_id=line_peer(d), device_id_type=MESH)

    pl.semaphore_wait(barrier, 30)

    roles, weights = [], []
    for p in range(PAIRS):
        charge = charges[p]
        roles.append(jnp.where(core == 0, charge, 2 - charge))
        weights.append(coupling[0, charge].astype(F32))

    def gathering(app):
        block = v.at[app]
        sends = []

        def unit_of(role, wave):
            cols = pl.ds(wave * CW, CW)
            if role == OUTER:
                first = lambda i, h: block.at[role, h, y, i, :, cols]
                second = lambda i, h: block.at[role, h, i, :, :, cols]
                return (("x", x, first), ("y", y, second))
            first = lambda i, h: block.at[role, h, i, x, :, cols]
            second = lambda i, h: block.at[role, h, :, i, :, cols]
            return (("y", y, first), ("x", x, second))

        def ring(role, wave, phase):
            axis, i, unit = unit_of(role, wave)[phase]
            right, left = lax.rem(i + 1, 4), lax.rem(i + 3, 4)
            send, recv = ring_s.at[wave, role, phase], ring_r.at[wave, role, phase]

            def mk(ref, device, k):
                return copy(ref, ref, send.at[k], recv.at[k], {axis: device})

            first = [
                mk(unit(i, 0), right, 0),
                mk(unit(i, 1), left, 1),
                mk(unit(i, 1), right, 2),
                mk(unit(i, 0), left, 3),
            ]
            onward = [mk(unit(left, 0), right, 4), mk(unit(right, 1), left, 5)]
            return first, onward

        def wave_steps(wave):
            cols = pl.ds(wave * CW, CW)
            mine = block.at[OWN, zl, y, x, :, cols]
            zc = [copy(mine, mine, z_s.at[wave, 0], z_r.at[wave, 0], {"zl": 1 - zl})]
            for q in range(2):
                zc.append(
                    copy(
                        mine,
                        block.at[OUTER, zl, y, x, :, cols],
                        z_s.at[wave, 1 + q],
                        z_r.at[wave, 1 + zl],
                        {"zl": q, "zh": far, "core": 1 - core},
                    )
                )
            rings = [[ring(r, wave, ph) for r in (OUTER, OWN)] for ph in range(2)]
            onto = copy(
                block.at[OWN, :, :, :, :, cols],
                block.at[OTHER, :, :, :, :, cols],
                other_s.at[wave],
                other_r.at[wave],
                {"core": 1 - core},
            )

            def s0():
                for c in zc:
                    c.start()
                sends.extend(zc)

            def start(phase):
                for k in range(4):
                    for first, _ in rings[phase]:
                        first[k].start()
                        sends.append(first[k])

            def onward(phase):
                for k in range(2):
                    for first, fwd in rings[phase]:
                        first[k].wait_recv()
                        fwd[k].start()
                        sends.append(fwd[k])

            def finish(phase, which):
                first, fwd = rings[phase][which]
                for c in (first[2], first[3], fwd[0], fwd[1]):
                    c.wait_recv()

            def s1():
                zc[0].wait_recv()
                for q in range(2):
                    there = block.at[OUTER, q, y, x, :, cols]
                    copy(
                        there, there, z_s.at[wave, 1 + q], z_r.at[wave, 1 + q], {"zl": 1 - zl}
                    ).wait_recv()
                start(0)

            def s3():
                finish(0, 0)
                finish(0, 1)
                start(1)

            def s5():
                finish(1, 1)
                onto.start()
                sends.append(onto)

            def s6():
                finish(1, 0)

            return [s0, s1, lambda: onward(0), s3, lambda: onward(1), s5, s6, onto.wait_recv]

        return [wave_steps(w) for w in range(WAVES)], sends

    def summing(app):
        sends = []

        def pieces(role, wave):
            cols = pl.ds(wave * CW, CW)
            if role == OUTER:
                first = lambda d, h: tsum.at[role, h, d, :, :, cols]
                second = lambda d, h: tsum.at[role, h, y, d, :, cols]
                return (("y", y, first), ("x", x, second))
            first = lambda d, h: tsum.at[role, h, :, d, :, cols]
            second = lambda d, h: tsum.at[role, h, d, x, :, cols]
            return (("x", x, first), ("y", y, second))

        def ring(role, wave, phase):
            axis, i, chunk = pieces(role, wave)[phase]
            right, left, opposite = lax.rem(i + 1, 4), lax.rem(i + 3, 4), lax.rem(i + 2, 4)
            send, recv = rring_s.at[wave, role, phase], rring_r.at[wave, role, phase]
            half = (bulk_half, tail_half)[phase].at[wave, role]
            full = (bulk_full, tail_full)[phase].at[wave, role]

            def mk(src, dst, device, k):
                return copy(src, dst, send.at[k], recv.at[k], {axis: device})

            first = [
                mk(chunk(opposite, 0), half.at[0], right, 0),
                mk(chunk(opposite, 1), half.at[1], left, 1),
                mk(chunk(right, 1), full.at[0, 1], right, 2),
                mk(chunk(left, 0), full.at[1, 0], left, 3),
            ]
            onward = [
                mk(chunk(right, 0), full.at[0, 0], right, 4),
                mk(chunk(left, 1), full.at[1, 1], left, 5),
            ]

            def pass_on(k):
                first[k].wait_recv()
                mine = chunk(right, 0) if k == 0 else chunk(left, 1)
                mine[...] += half[k]
                onward[k].start()
                sends.append(onward[k])

            def finish():
                for c in (first[2], first[3], onward[0], onward[1]):
                    c.wait_recv()
                for h in range(2):
                    mine = chunk(i, h)
                    mine[...] += full[0, h] + full[1, h]

            return first, pass_on, finish

        def wave_steps(wave):
            cols = pl.ds(wave * CW, CW)
            rings = [[ring(r, wave, ph) for r in (OUTER, OWN)] for ph in range(2)]
            onto = copy(
                tsum.at[OTHER, :, :, :, :, cols],
                otherbuf.at[wave],
                rother_s.at[wave],
                rother_r.at[wave],
                {"core": 1 - core},
            )
            zc = [
                copy(
                    tsum.at[OWN, 1 - zl, y, x, :, cols],
                    zbuf.at[wave, 0],
                    rz_s.at[wave, 0],
                    rz_r.at[wave, 0],
                    {"zl": 1 - zl},
                )
            ]
            for q in range(2):
                zc.append(
                    copy(
                        tsum.at[OUTER, q, y, x, :, cols],
                        zbuf.at[wave, 1 + zl],
                        rz_s.at[wave, 1 + q],
                        rz_r.at[wave, 1 + zl],
                        {"zl": q, "zh": far, "core": 1 - core},
                    )
                )

            def start(phase, which):
                for c in rings[phase][which][0]:
                    c.start()
                    sends.append(c)

            def pass_on(phase):
                for k in range(2):
                    for r in rings[phase]:
                        r[1](k)

            def give_other():
                onto.start()
                sends.append(onto)

            def middle():
                rings[0][0][2]()
                start(1, 0)
                rings[0][1][2]()
                start(1, 1)

            def last():
                rings[1][0][2]()
                rings[1][1][2]()
                for c in zc:
                    c.start()
                sends.extend(zc)

            def collect():
                zc[0].wait_recv()
                for q in range(2):
                    copy(
                        tsum.at[OUTER, q, y, x, :, cols],
                        zbuf.at[wave, 1 + q],
                        rz_s.at[wave, 1 + q],
                        rz_r.at[wave, 1 + q],
                        {"zl": 1 - zl},
                    ).wait_recv()
                image[:, cols] = (tsum[OWN, zl, y, x, :, cols] + zbuf[wave, 0]) + (
                    zbuf[wave, 1] + zbuf[wave, 2]
                )

            return {
                "outer": lambda: start(0, 0),
                "own": lambda: start(0, 1),
                "other": give_other,
                "take": onto.wait_recv,
                "steps": [
                    lambda: pass_on(0),
                    middle,
                    lambda: pass_on(1),
                    last,
                    collect,
                ],
            }

        return [wave_steps(w) for w in range(WAVES)], sends

    def reduction(k, stage, tile):
        place = places[stage]
        buf = arbuf.at[k, stage]
        buf[place] = tile

        def one(d):
            mine = buf.at[place]
            return copy(mine, mine, ar_s.at[k, stage], ar_r.at[k, stage], peers[stage](d))

        @pl.loop(1, 16)
        def _(d):
            one(d).start()

        def finish():
            many = buf.at[pl.ds(0, 15)]
            waited = copy(many, many, ar_s.at[k, stage], ar_r.at[k, stage], peers[stage](1))
            waited.wait_recv()
            waited.wait_send()
            return jnp.sum(buf[...], axis=0)

        return finish

    def packed(*values):
        row = lax.broadcasted_iota(jnp.int32, TILE, 0)
        tile = jnp.zeros(TILE, F32)
        for k, value in enumerate(values):
            tile = jnp.where(row == k, value, tile)
        return tile

    def prepare():
        for p in range(PAIRS):
            for c in loads[p]:
                c.wait()

        @pl.loop(0, PAIRS * 4)
        def _(step):
            p = step // 4
            at = pl.multiple_of(lax.rem(step, 4) * 128, 128)
            at2 = pl.multiple_of(at + M, 128)
            at3 = pl.multiple_of(at + 2 * M, 128)
            rows = pl.ds(at, 128)
            left_rows, right_rows = raw[0, p, rows, :], raw[1, p, rows, :]
            hi, lo = split(left_rows)
            lcat[p, rows, 0:M] = hi
            lcat[p, rows, M : 2 * M] = hi
            lcat[p, rows, 2 * M :] = lo
            hi, lo = split(left_rows.T)
            ltcat[p, :, rows] = hi
            ltcat[p, :, pl.ds(at2, 128)] = hi
            ltcat[p, :, pl.ds(at3, 128)] = lo
            hi, lo = split(right_rows)
            rcat[p, rows, :] = hi
            rcat[p, pl.ds(at2, 128), :] = hi
            rcat[p, pl.ds(at3, 128), :] = lo
            hi, lo = split(right_rows.T)
            for third, part in enumerate((hi, hi, lo)):
                rtcat[p, third * M : (third + 1) * M, rows] = part

    def halve(app, role, wave):
        cols = pl.ds(wave * CW, CW)

        @pl.loop(0, 8)
        def _(step):
            h, j = step // 4, lax.rem(step, 4)
            at = pl.multiple_of(step * 64, 64)
            hi, lo = split(v[app, role, h, j, :, :, cols].reshape(64, CW))
            vcat[role, pl.ds(at, 64), cols] = hi
            vcat[role, pl.ds(pl.multiple_of(at + M, 64), 64), cols] = lo
            vcat[role, pl.ds(pl.multiple_of(at + 2 * M, 64), 64), cols] = hi

    def first_products(wave, forward):
        cols = pl.ds(wave * CW, CW)
        for p in range(PAIRS):
            if forward:
                hi, lo = split(dot(lcat[p], vcat[OWN, :, cols]))
                into = ycat
            else:
                hi, lo = split(weights[p] * dot(ltcat[p], vcat[roles[p], :, cols]))
                into = zcat
            for third, part in enumerate((hi, lo, hi)):
                into[p, :, third * M + wave * CW : third * M + (wave + 1) * CW] = part

    def forward_terms(app, wave):
        cols = pl.ds(wave * CW, CW)
        for p in range(PAIRS):
            fbuf[p] = dot(ycat[p], rtcat[p, :, cols])
        factors = [
            [jnp.where(roles[p] == r, weights[p], 0.0) for p in range(PAIRS)] for r in range(3)
        ]

        def body(step, acc):
            h, j = step // 4, lax.rem(step, 4)
            rows = pl.ds(pl.multiple_of(step * 64, 64), 64)
            f = [fbuf[p, rows, :] for p in range(PAIRS)]
            for r in range(3):
                term = factors[r][0] * f[0] + factors[r][1] * f[1] + factors[r][2] * f[2]
                tsum[r, h, j, :, :, cols] = term.reshape(4, ROWS, CW)
                both = term * v[app, r, h, j, :, :, cols].reshape(64, CW)
                acc = acc + jnp.sum(both.reshape(8, 8, CW), axis=0)
            return acc

        return lax.fori_loop(0, 8, body, jnp.zeros((8, CW), F32))

    def backward_terms(wave):
        cols = pl.ds(wave * CW, CW)
        for p in range(PAIRS):
            fbuf[p] = dot(zcat[p], rcat[p, :, cols])

    def join(wave):
        cols = pl.ds(wave * CW, CW)

        @pl.loop(0, 8)
        def _(step):
            h, j = step // 4, lax.rem(step, 4)
            rows = pl.ds(pl.multiple_of(step * 64, 64), 64)
            back = fbuf[0, rows, :] + fbuf[1, rows, :] + fbuf[2, rows, :]
            tsum[OWN, h, j, :, :, cols] += (
                back.reshape(4, ROWS, CW) + otherbuf[wave, h, j]
            )

    def apply(app, source, before, extra):
        v[app, OWN, zl, y, x] = source
        waves, gather_sends = gathering(app)
        for k in range(2):
            for steps in waves:
                steps[k]()
            if k == 0:
                before()
        for k in range(2, 8):
            for w, steps in enumerate(waves):
                steps[k]()
        for w in range(WAVES):
            for r in range(3):
                halve(app, r, w)
            first_products(w, True)
            first_products(w, False)
        waves, sum_sends = summing(app)
        parts = []
        for w, steps in enumerate(waves):
            parts.append(forward_terms(app, w))
            steps["other"]()
            steps["outer"]()
            backward_terms(w)
            steps["take"]()
            join(w)
            steps["own"]()
        partial = 2.0 * sum(total(part) for part in parts)
        finish = extra(partial)
        for k in range(5):
            for steps in waves:
                steps["steps"][k]()
            if k == 1:
                finish = reduction(2 * app, 1, finish())
        for c in gather_sends + sum_sends:
            c.wait_send()
        return finish()

    w = w_in[...]
    norm_part = total(w * w)
    sums = apply(0, w, prepare, lambda part: reduction(0, 0, packed(norm_part, part)))
    norm_sq, correlation = sums[0:1, 0:1], sums[1:2, 0:1]
    theta = correlation / norm_sq
    inverse = lax.rsqrt(norm_sq)
    vector = w * inverse
    first = image[...] * inverse
    correction = (first - theta * vector) / pre_in[...]
    corrected[...] = correction
    image_out[...] = first
    finish = reduction(
        1,
        0,
        packed(
            total(vector * correction), total(correction * correction), total(first * correction)
        ),
    )
    held = []

    def second_extra(part):
        held.append(reduction(1, 1, finish()))
        return reduction(2, 0, packed(part))

    sums = apply(1, correction, lambda: None, second_extra)
    product = sums[0:1, 0:1]
    sums = held[0]()
    along, squared, with_image = sums[0:1, 0:1], sums[1:2, 0:1], sums[2:3, 0:1]
    length_sq = squared - along * along
    scale_back = lax.rsqrt(length_sq + 1e-30)
    corner = (
        scale_back * scale_back * (product - 2.0 * along * with_image + along * along * theta)
    )
    cross = scale_back * (with_image - along * theta)
    half = (theta - corner) / 2.0
    lowest = (theta + corner) / 2.0 - jnp.sqrt(half * half + cross * cross)
    u1 = corner - lowest
    u2 = -cross
    size_norm = jnp.sqrt(u1 * u1 + u2 * u2 + 1e-30)
    scale = math.sqrt(8 * M * M)
    one, two = scale * u1 / size_norm, scale * u2 / size_norm
    vector = w_in[...] * inverse
    first = image_out[...]
    basis = (corrected[...] - along * vector) * scale_back
    second = (image[...] - along * first) * scale_back
    state_out[...] = one * vector + two * basis
    image_out[...] = one * first + two * second
    energy_out[...] = packed(theta, lowest)


def per_device(wavefunction, preconditioner, left_ops, right_ops, charges, coupling):
    rows = jax.ShapeDtypeStruct((ROWS, M), F32)
    vmem = pl.BlockSpec(memory_space=pltpu.VMEM)
    smem = pl.BlockSpec(memory_space=pltpu.SMEM)
    dma = pltpu.SemaphoreType.DMA
    state, image, energies = pl.pallas_call(
        kernel,
        out_shape=(rows, rows, jax.ShapeDtypeStruct(TILE, F32)),
        in_specs=[smem, smem, vmem, vmem]
        + [pl.BlockSpec(memory_space=pl.ANY)] * 2,
        out_specs=(vmem, vmem, vmem),
        scratch_shapes=[
            pltpu.VMEM((2, PAIRS, M, M), F32),
            pltpu.VMEM((PAIRS, M, 3 * M), BF16),
            pltpu.VMEM((PAIRS, M, 3 * M), BF16),
            pltpu.VMEM((PAIRS, 3 * M, M), BF16),
            pltpu.VMEM((PAIRS, 3 * M, M), BF16),
            pltpu.VMEM((2, 3, 2, 4, 4, ROWS, M), F32),
            pltpu.VMEM((3, 3 * M, M), BF16),
            pltpu.VMEM((PAIRS, M, 3 * M), BF16),
            pltpu.VMEM((PAIRS, M, 3 * M), BF16),
            pltpu.VMEM((PAIRS, M, CW), F32),
            pltpu.VMEM((3, 2, 4, 4, ROWS, M), F32),
            pltpu.VMEM((WAVES, 2, 4, 4, ROWS, CW), F32),
            pltpu.VMEM((WAVES, 2, 2, 4, ROWS, CW), F32),
            pltpu.VMEM((WAVES, 2, 2, 2, 4, ROWS, CW), F32),
            pltpu.VMEM((WAVES, 2, 2, ROWS, CW), F32),
            pltpu.VMEM((WAVES, 2, 2, 2, ROWS, CW), F32),
            pltpu.VMEM((WAVES, 3, ROWS, CW), F32),
            pltpu.VMEM((ROWS, M), F32),
            pltpu.VMEM((ROWS, M), F32),
            pltpu.VMEM((3, 2, 16) + TILE, F32),
            dma((2, PAIRS)),
            dma((WAVES, 3)),
            dma((WAVES, 3)),
            dma((WAVES, 2, 2, 6)),
            dma((WAVES, 2, 2, 6)),
            dma((WAVES,)),
            dma((WAVES,)),
            dma((WAVES, 3)),
            dma((WAVES, 3)),
            dma((WAVES, 2, 2, 6)),
            dma((WAVES, 2, 2, 6)),
            dma((WAVES,)),
            dma((WAVES,)),
            dma((3, 2)),
            dma((3, 2)),
        ],
        compiler_params=pltpu.CompilerParams(
            collective_id=0, has_side_effects=True, vmem_limit_bytes=60 * 1024 * 1024
        ),
    )(
        charges,
        coupling,
        wavefunction.reshape(ROWS, M),
        preconditioner.reshape(ROWS, M),
        left_ops.reshape(PAIRS, M, M),
        right_ops.reshape(PAIRS, M, M),
    )
    return state.reshape(1, ROWS, M), image.reshape(1, ROWS, M), energies[0:2, 0]


def solution(mesh):
    split_mesh = Mesh(mesh.devices.reshape(2, 4, 4, 4, 2), PAIR + SECTOR)
    placed = (
        P(SECTOR, PAIR, None),
        P(SECTOR, PAIR, None),
        P(PAIR, SECTOR, None, None),
        P(PAIR, SECTOR, None, None),
        P(PAIR),
        P(SECTOR, None),
    )
    return jax.shard_map(
        per_device,
        mesh=split_mesh,
        in_specs=placed,
        out_specs=(P(SECTOR, PAIR, None), P(SECTOR, PAIR, None), P()),
        check_vma=False,
    )
```

```python
import math

import jax
import jax.numpy as jnp
from jax import lax
from jax.experimental import pallas as pl
from jax.experimental.pallas import tpu as pltpu
from jax.sharding import Mesh
from jax.sharding import PartitionSpec as P

SECTOR = ("zh", "core")
PAIR = ("zl", "y", "x")
MESH = pl.DeviceIdType.MESH
F32 = jnp.float32
BF16 = jnp.bfloat16

M = 512
ROWS = 16
PAIRS = 3
OUTER, OWN, OTHER = 0, 1, 2
WAVES = 2
CW = M // WAVES
TILE = (8, 128)


def split(x):
    high = x.astype(BF16)
    return high, (x - high.astype(F32)).astype(BF16)


def total(x):
    return jnp.sum(jnp.sum(x, axis=0, keepdims=True), axis=1, keepdims=True)


def dot(a, b):
    return jnp.dot(a, b, preferred_element_type=F32)


def kernel(
    charges,
    coupling,
    w_in,
    pre_in,
    l_hbm,
    r_hbm,
    packed_out,
    raw,
    lcat,
    ltcat,
    rcat,
    rtcat,
    v,
    vcat,
    ycat,
    zcat,
    fbuf,
    tsum,
    otherbuf,
    bulk_half,
    bulk_full,
    tail3,
    tail7,
    tail2,
    image,
    corrected,
    held,
    arbuf,
    load_sem,
    z_s,
    z_r,
    ring_s,
    ring_r,
    other_s,
    other_r,
    rz_s,
    rz_r,
    rring_s,
    rring_r,
    rother_s,
    rother_r,
    ar_s,
    ar_r,
):
    zl, y, x = (lax.axis_index(a) for a in PAIR)
    zh, core = (lax.axis_index(a) for a in SECTOR)
    far = lax.rem(zh + 2 * core + 3, 4)
    places = (x, zl * 4 + y, zh * 2 + core)
    sizes = (4, 8, 8)

    def along_x(d):
        return {"x": lax.rem(x + d, 4)}

    def along_y(d):
        return {"y": lax.rem(y + d, 4)}

    def along_yz(d):
        place = lax.rem(places[1] + d, 8)
        return {"zl": place // 4, "y": lax.rem(place, 4)}

    def along_sector(d):
        place = lax.rem(places[2] + d, 8)
        return {"zh": place // 2, "core": lax.rem(place, 2)}

    peers = (along_x, along_yz, along_sector)

    def copy(src, dst, send, recv, device):
        return pltpu.make_async_remote_copy(
            src_ref=src,
            dst_ref=dst,
            send_sem=send,
            recv_sem=recv,
            device_id=device,
            device_id_type=MESH,
        )

    loads = []
    for p in range(PAIRS):
        loads.append(
            (
                pltpu.make_async_copy(l_hbm.at[p], raw.at[0, p], load_sem.at[0, p]),
                pltpu.make_async_copy(r_hbm.at[p], raw.at[1, p], load_sem.at[1, p]),
            )
        )
        for c in loads[-1]:
            c.start()

    barrier = pltpu.get_barrier_semaphore()
    signals = [g(d) for g, n in zip(peers, sizes) for d in range(1, n)]
    signals.append({"zl": 1 - zl, "zh": far, "core": 1 - core})
    for device in signals:
        pl.semaphore_signal(barrier, inc=1, device_id=device, device_id_type=MESH)

    roles, weights = [], []
    for p in range(PAIRS):
        charge = charges[p]
        roles.append(jnp.where(core == 0, charge, 2 - charge))
        weights.append(coupling[0, charge].astype(F32))

    def gathering(app):
        block = v.at[app]
        sends = []

        def begin(copies):
            for c in copies:
                c.start()
            sends.extend(copies)

        def wave_steps(wave):
            cols = pl.ds(wave * CW, CW)
            mine = block.at[OWN, zl, y, x, :, cols]

            def ring(phase, ref, group, n):
                return [
                    copy(
                        ref,
                        ref,
                        ring_s.at[wave, phase, d - 1],
                        ring_r.at[wave, phase, d - 1],
                        group(d),
                    )
                    for d in range(1, n)
                ]

            across = [
                copy(
                    mine,
                    block.at[OUTER, zl, y, x, :, cols],
                    z_s.at[wave, q],
                    z_r.at[wave, zl],
                    {"zl": q, "zh": far, "core": 1 - core},
                )
                for q in range(2)
            ]
            own1 = ring(0, mine, along_yz, 8)
            outer1 = ring(2, block.at[OUTER, :, y, x, :, cols], along_x, 4)

            def two_way(phase, unit, i, group):
                def one(ref, d, k):
                    return copy(
                        ref, ref, ring_s.at[wave, phase, k], ring_r.at[wave, phase, k], group(d)
                    )

                first = [
                    one(unit(i, 0), 1, 0),
                    one(unit(i, 1), 3, 1),
                    one(unit(i, 1), 1, 2),
                    one(unit(i, 0), 3, 3),
                ]
                onward = [
                    one(unit(lax.rem(i + 3, 4), 0), 1, 4),
                    one(unit(lax.rem(i + 1, 4), 1), 3, 5),
                ]
                return first, onward

            own2, own2_on = two_way(1, lambda i, h: block.at[OWN, h, :, i, :, cols], x, along_x)
            outer2, outer2_on = two_way(
                3, lambda i, h: block.at[OUTER, h, i, :, :, cols], y, along_y
            )
            onto = copy(
                block.at[OWN, :, :, :, :, cols],
                block.at[OTHER, :, :, :, :, cols],
                other_s.at[wave],
                other_r.at[wave],
                {"core": 1 - core},
            )

            def arrived(copies):
                for c in copies:
                    c.wait_recv()

            def outer_first():
                for q in range(2):
                    there = block.at[OUTER, q, y, x, :, cols]
                    copy(
                        there, there, z_s.at[wave, q], z_r.at[wave, q], {"zl": 1 - zl}
                    ).wait_recv()
                begin(outer1)

            def own_second():
                arrived(own1)
                begin(own2)

            def outer_second():
                arrived(outer1)
                begin(outer2)

            def pass_on(first, onward):
                for k in range(2):
                    first[k].wait_recv()
                    begin([onward[k]])

            def hand_over():
                arrived(own2[2:] + own2_on)
                begin([onto])

            return {
                "across": lambda: begin(across),
                "own1": lambda: begin(own1),
                "outer1": outer_first,
                "own2": own_second,
                "outer2": outer_second,
                "own": hand_over,
                "own2_on": lambda: pass_on(own2, own2_on),
                "outer2_on": lambda: pass_on(outer2, outer2_on),
                "outer": lambda: arrived(outer2[2:] + outer2_on),
                "other": onto.wait_recv,
            }

        return [wave_steps(w) for w in range(WAVES)], sends

    def summing(app):
        sends = []

        def begin(copies):
            for c in copies:
                c.start()
            sends.extend(copies)

        def arrived(copies):
            for c in copies:
                c.wait_recv()

        def wave_steps(wave):
            cols = pl.ds(wave * CW, CW)

            def ring(phase, chunk, into, group, n):
                return [
                    copy(
                        chunk(d),
                        into.at[d - 1],
                        rring_s.at[wave, phase, d - 1],
                        rring_r.at[wave, phase, d - 1],
                        group(d),
                    )
                    for d in range(1, n)
                ]

            small_outer, small_own, crossed = tail3.at[wave], tail7.at[wave], tail2.at[wave]
            def two_way(phase, chunk, half, full, i, group):
                def one(src, dst, d, k):
                    return copy(
                        src, dst, rring_s.at[wave, phase, k], rring_r.at[wave, phase, k], group(d)
                    )

                right, left, opposite = lax.rem(i + 1, 4), lax.rem(i + 3, 4), lax.rem(i + 2, 4)
                first = [
                    one(chunk(opposite, 0), half.at[0], 1, 0),
                    one(chunk(opposite, 1), half.at[1], 3, 1),
                    one(chunk(right, 1), full.at[0, 1], 1, 2),
                    one(chunk(left, 0), full.at[1, 0], 3, 3),
                ]
                onward = [
                    one(chunk(right, 0), full.at[0, 0], 1, 4),
                    one(chunk(left, 1), full.at[1, 1], 3, 5),
                ]

                def pass_on():
                    for k, mine in enumerate((chunk(right, 0), chunk(left, 1))):
                        first[k].wait_recv()
                        mine[...] += half[k]
                        begin([onward[k]])

                def finish():
                    arrived(first[2:] + onward)
                    for h in range(2):
                        mine = chunk(i, h)
                        mine[...] += full[0, h] + full[1, h]

                return first, pass_on, finish

            outer2, outer2_on, outer2_end = two_way(
                0,
                lambda d, h: tsum.at[OUTER, h, d, :, :, cols],
                bulk_half.at[wave, 0],
                bulk_full.at[wave, 0],
                y,
                along_y,
            )
            own2, own2_on, own2_end = two_way(
                1,
                lambda d, h: tsum.at[OWN, h, :, d, :, cols],
                bulk_half.at[wave, 1],
                bulk_full.at[wave, 1],
                x,
                along_x,
            )
            outer1 = ring(
                2,
                lambda d: tsum.at[OUTER, :, y, lax.rem(x + d, 4), :, cols],
                small_outer,
                along_x,
                4,
            )

            def to_yz(d):
                place = lax.rem(places[1] + d, 8)
                return tsum.at[OWN, place // 4, lax.rem(place, 4), x, :, cols]

            own1 = ring(3, to_yz, small_own, along_yz, 8)
            across = [
                copy(
                    tsum.at[OUTER, q, y, x, :, cols],
                    crossed.at[zl],
                    rz_s.at[wave, q],
                    rz_r.at[wave, zl],
                    {"zl": q, "zh": far, "core": 1 - core},
                )
                for q in range(2)
            ]
            onto = copy(
                tsum.at[OTHER, :, :, :, :, cols],
                otherbuf.at[wave],
                rother_s.at[wave],
                rother_r.at[wave],
                {"core": 1 - core},
            )

            def outer_first():
                outer2_end()
                begin(outer1)

            def own_first():
                own2_end()
                begin(own1)

            def outer_across():
                arrived(outer1)
                tsum[OUTER, :, y, x, :, cols] += small_outer[0] + (
                    small_outer[1] + small_outer[2]
                )
                begin(across)

            def own_done():
                arrived(own1)
                image[:, cols] = tsum[OWN, zl, y, x, :, cols] + jnp.sum(small_own[...], axis=0)

            def collect():
                for q in range(2):
                    copy(
                        tsum.at[OUTER, q, y, x, :, cols],
                        crossed.at[q],
                        rz_s.at[wave, q],
                        rz_r.at[wave, q],
                        {"zl": 1 - zl},
                    ).wait_recv()
                image[:, cols] += crossed[0] + crossed[1]

            return {
                "outer2": lambda: begin(outer2),
                "own2": lambda: begin(own2),
                "other": lambda: begin([onto]),
                "take": onto.wait_recv,
                "outer2_on": outer2_on,
                "own2_on": own2_on,
                "outer1": outer_first,
                "own1": own_first,
                "across": outer_across,
                "own": own_done,
                "collect": collect,
            }

        return [wave_steps(w) for w in range(WAVES)], sends

    class Reduction:
        def __init__(self, k, tile):
            self.k, self.stage = k, 0
            self.send(tile)

        def send(self, tile):
            stage, place = self.stage, places[self.stage]
            self.buf = arbuf.at[self.k, stage]
            self.buf[place] = tile
            mine = self.buf.at[place]
            for d in range(1, sizes[stage]):
                copy(
                    mine,
                    mine,
                    ar_s.at[self.k, stage],
                    ar_r.at[self.k, stage],
                    peers[stage](d),
                ).start()

        def step(self):
            stage, n = self.stage, sizes[self.stage]
            many = self.buf.at[pl.ds(0, n - 1)]
            waited = copy(
                many, many, ar_s.at[self.k, stage], ar_r.at[self.k, stage], peers[stage](1)
            )
            waited.wait_recv()
            waited.wait_send()
            tile = jnp.sum(self.buf[pl.ds(0, n)], axis=0)
            self.stage += 1
            if self.stage < 3:
                self.send(tile)
            return tile

    def packed(*values):
        row = lax.broadcasted_iota(jnp.int32, TILE, 0)
        tile = jnp.zeros(TILE, F32)
        for k, value in enumerate(values):
            tile = jnp.where(row == k, value, tile)
        return tile

    def prepare():
        for p in range(PAIRS):
            for c in loads[p]:
                c.wait()

        @pl.loop(0, PAIRS * 4)
        def _(step):
            p = step // 4
            at = pl.multiple_of(lax.rem(step, 4) * 128, 128)
            at2 = pl.multiple_of(at + M, 128)
            at3 = pl.multiple_of(at + 2 * M, 128)
            rows = pl.ds(at, 128)
            left_rows, right_rows = raw[0, p, rows, :], raw[1, p, rows, :]
            hi, lo = split(left_rows)
            lcat[p, rows, 0:M] = hi
            lcat[p, rows, M : 2 * M] = hi
            lcat[p, rows, 2 * M :] = lo
            hi, lo = split(left_rows.T)
            ltcat[p, :, rows] = hi
            ltcat[p, :, pl.ds(at2, 128)] = hi
            ltcat[p, :, pl.ds(at3, 128)] = lo
            hi, lo = split(right_rows)
            rcat[p, rows, :] = hi
            rcat[p, pl.ds(at2, 128), :] = hi
            rcat[p, pl.ds(at3, 128), :] = lo
            hi, lo = split(right_rows.T)
            for third, part in enumerate((hi, hi, lo)):
                rtcat[p, third * M : (third + 1) * M, rows] = part

    def halve(app, role, wave):
        cols = pl.ds(wave * CW, CW)

        @pl.loop(0, 8)
        def _(step):
            h, j = step // 4, lax.rem(step, 4)
            at = pl.multiple_of(step * 64, 64)
            hi, lo = split(v[app, role, h, j, :, :, cols].reshape(64, CW))
            vcat[role, pl.ds(at, 64), cols] = hi
            vcat[role, pl.ds(pl.multiple_of(at + M, 64), 64), cols] = lo
            vcat[role, pl.ds(pl.multiple_of(at + 2 * M, 64), 64), cols] = hi

    def first_products(wave, forward):
        cols = pl.ds(wave * CW, CW)
        for p in range(PAIRS):
            if forward:
                hi, lo = split(dot(lcat[p], vcat[OWN, :, cols]))
                into = ycat
            else:
                hi, lo = split(weights[p] * dot(ltcat[p], vcat[roles[p], :, cols]))
                into = zcat
            for third, part in enumerate((hi, lo, hi)):
                into[p, :, third * M + wave * CW : third * M + (wave + 1) * CW] = part

    def forward_terms(app, wave):
        cols = pl.ds(wave * CW, CW)
        for p in range(PAIRS):
            fbuf[p] = dot(ycat[p], rtcat[p, :, cols])
        factors = [
            [jnp.where(roles[p] == r, weights[p], 0.0) for p in range(PAIRS)] for r in range(3)
        ]

        def body(step, acc):
            h, j = step // 4, lax.rem(step, 4)
            rows = pl.ds(pl.multiple_of(step * 64, 64), 64)
            f = [fbuf[p, rows, :] for p in range(PAIRS)]
            for r in range(3):
                term = factors[r][0] * f[0] + factors[r][1] * f[1] + factors[r][2] * f[2]
                tsum[r, h, j, :, :, cols] = term.reshape(4, ROWS, CW)
                both = term * v[app, r, h, j, :, :, cols].reshape(64, CW)
                acc = acc + jnp.sum(both.reshape(8, 8, CW), axis=0)
            return acc

        return lax.fori_loop(0, 8, body, jnp.zeros((8, CW), F32))

    def backward_terms(wave):
        cols = pl.ds(wave * CW, CW)
        for p in range(PAIRS):
            fbuf[p] = dot(zcat[p], rcat[p, :, cols])

    def join(wave):
        cols = pl.ds(wave * CW, CW)

        @pl.loop(0, 8)
        def _(step):
            h, j = step // 4, lax.rem(step, 4)
            rows = pl.ds(pl.multiple_of(step * 64, 64), 64)
            back = fbuf[0, rows, :] + fbuf[1, rows, :] + fbuf[2, rows, :]
            tsum[OWN, h, j, :, :, cols] += (
                back.reshape(4, ROWS, CW) + otherbuf[wave, h, j]
            )

    def apply(app, source, scalars):
        v[app, OWN, zl, y, x] = source
        waves, gather_sends = gathering(app)
        for step in ("across", "own1"):
            for g in waves:
                g[step]()
        values = scalars()
        beside = Reduction(1, packed(*values)) if app else None
        for g in waves:
            g["outer1"]()
        for g in waves:
            g["own2"]()
        for g in waves:
            g["outer2"]()
        for g in waves:
            g["own2_on"]()
            g["outer2_on"]()
        if beside:
            beside.step()
        for w, g in enumerate(waves):
            g["own"]()
            halve(app, OWN, w)
            first_products(w, True)
        if beside:
            beside.step()
        for w, g in enumerate(waves):
            g["other"]()
            halve(app, OTHER, w)
            g["outer"]()
            halve(app, OUTER, w)
            first_products(w, False)
        beside = beside.step() if beside else None
        waves, sum_sends = summing(app)
        parts = []
        for w, g in enumerate(waves):
            parts.append(forward_terms(app, w))
            g["other"]()
            g["outer2"]()
            if w == WAVES - 1:
                partial = 2.0 * sum(total(part) for part in parts)
                full = Reduction(2 * app, packed(partial, *(() if app else values)))
            backward_terms(w)
            g["take"]()
            join(w)
            g["own2"]()
            if w:
                waves[w - 1]["outer2_on"]()
                waves[w - 1]["own2_on"]()
        waves[-1]["outer2_on"]()
        waves[-1]["own2_on"]()
        full.step()
        for g in waves[:-1]:
            g["outer1"]()
            g["own1"]()
        waves[-1]["outer1"]()
        waves[-1]["own1"]()
        full.step()
        for g in waves:
            g["across"]()
        for g in waves:
            g["own"]()
        result = full.step()
        for g in waves:
            g["collect"]()
        for c in gather_sends + sum_sends:
            c.wait_send()
        return result, beside

    prepare()
    pl.semaphore_wait(barrier, len(signals))
    w = w_in[...]
    sums, _ = apply(0, w, lambda: (total(w * w),))
    correlation, norm_sq = sums[0:1, 0:1], sums[1:2, 0:1]
    theta = correlation / norm_sq
    inverse = lax.rsqrt(norm_sq)
    vector = w * inverse
    first = image[...] * inverse
    correction = (first - theta * vector) / pre_in[...]
    corrected[...] = correction
    held[...] = first
    sums, beside = apply(
        1,
        correction,
        lambda: (
            total(vector * correction),
            total(correction * correction),
            total(first * correction),
        ),
    )
    product = sums[0:1, 0:1]
    along, squared, with_image = beside[0:1, 0:1], beside[1:2, 0:1], beside[2:3, 0:1]
    length_sq = squared - along * along
    scale_back = lax.rsqrt(length_sq + 1e-30)
    corner = (
        scale_back * scale_back * (product - 2.0 * along * with_image + along * along * theta)
    )
    cross = scale_back * (with_image - along * theta)
    half = (theta - corner) / 2.0
    lowest = (theta + corner) / 2.0 - jnp.sqrt(half * half + cross * cross)
    u1 = corner - lowest
    u2 = -cross
    size_norm = jnp.sqrt(u1 * u1 + u2 * u2 + 1e-30)
    scale = math.sqrt(8 * M * M)
    one, two = scale * u1 / size_norm, scale * u2 / size_norm
    vector = w_in[...] * inverse
    first = held[...]
    basis = (corrected[...] - along * vector) * scale_back
    second = (image[...] - along * first) * scale_back
    packed_out[0:ROWS, :] = one * vector + two * basis
    packed_out[ROWS : 2 * ROWS, :] = one * first + two * second
    packed_out[2 * ROWS :, 0:128] = packed(theta, lowest)


def per_device(wavefunction, preconditioner, left_ops, right_ops, charges, coupling):
    vmem = pl.BlockSpec(memory_space=pltpu.VMEM)
    smem = pl.BlockSpec(memory_space=pltpu.SMEM)
    dma = pltpu.SemaphoreType.DMA
    out = pl.pallas_call(
        kernel,
        out_shape=jax.ShapeDtypeStruct((2 * ROWS + 8, M), F32),
        in_specs=[smem, smem, vmem, vmem]
        + [pl.BlockSpec(memory_space=pl.ANY)] * 2,
        out_specs=vmem,
        scratch_shapes=[
            pltpu.VMEM((2, PAIRS, M, M), F32),
            pltpu.VMEM((PAIRS, M, 3 * M), BF16),
            pltpu.VMEM((PAIRS, M, 3 * M), BF16),
            pltpu.VMEM((PAIRS, 3 * M, M), BF16),
            pltpu.VMEM((PAIRS, 3 * M, M), BF16),
            pltpu.VMEM((2, 3, 2, 4, 4, ROWS, M), F32),
            pltpu.VMEM((3, 3 * M, M), BF16),
            pltpu.VMEM((PAIRS, M, 3 * M), BF16),
            pltpu.VMEM((PAIRS, M, 3 * M), BF16),
            pltpu.VMEM((PAIRS, M, CW), F32),
            pltpu.VMEM((3, 2, 4, 4, ROWS, M), F32),
            pltpu.VMEM((WAVES, 2, 4, 4, ROWS, CW), F32),
            pltpu.VMEM((WAVES, 2, 2, 4, ROWS, CW), F32),
            pltpu.VMEM((WAVES, 2, 2, 2, 4, ROWS, CW), F32),
            pltpu.VMEM((WAVES, 3, 2, ROWS, CW), F32),
            pltpu.VMEM((WAVES, 7, ROWS, CW), F32),
            pltpu.VMEM((WAVES, 2, ROWS, CW), F32),
            pltpu.VMEM((ROWS, M), F32),
            pltpu.VMEM((ROWS, M), F32),
            pltpu.VMEM((ROWS, M), F32),
            pltpu.VMEM((3, 3, 8) + TILE, F32),
            dma((2, PAIRS)),
            dma((WAVES, 2)),
            dma((WAVES, 2)),
            dma((WAVES, 4, 7)),
            dma((WAVES, 4, 7)),
            dma((WAVES,)),
            dma((WAVES,)),
            dma((WAVES, 2)),
            dma((WAVES, 2)),
            dma((WAVES, 4, 7)),
            dma((WAVES, 4, 7)),
            dma((WAVES,)),
            dma((WAVES,)),
            dma((3, 3)),
            dma((3, 3)),
        ],
        compiler_params=pltpu.CompilerParams(
            collective_id=0, has_side_effects=True, vmem_limit_bytes=60 * 1024 * 1024
        ),
    )(
        charges,
        coupling,
        wavefunction.reshape(ROWS, M),
        preconditioner.reshape(ROWS, M),
        left_ops.reshape(PAIRS, M, M),
        right_ops.reshape(PAIRS, M, M),
    )
    return out[None, 0:ROWS], out[None, ROWS : 2 * ROWS], out[2 * ROWS : 2 * ROWS + 2, 0]


def solution(mesh):
    split_mesh = Mesh(mesh.devices.reshape(2, 4, 4, 4, 2), PAIR + SECTOR)
    placed = (
        P(SECTOR, PAIR, None),
        P(SECTOR, PAIR, None),
        P(PAIR, SECTOR, None, None),
        P(PAIR, SECTOR, None, None),
        P(PAIR),
        P(SECTOR, None),
    )
    return jax.shard_map(
        per_device,
        mesh=split_mesh,
        in_specs=placed,
        out_specs=(P(SECTOR, PAIR, None), P(SECTOR, PAIR, None), P()),
        check_vma=False,
    )
```

```python
import math

import jax
import jax.numpy as jnp
from jax import lax
from jax.experimental import pallas as pl
from jax.experimental.pallas import tpu as pltpu
from jax.sharding import Mesh
from jax.sharding import PartitionSpec as P

SECTOR = ("zh", "core")
PAIR = ("zl", "y", "x")
MESH = pl.DeviceIdType.MESH
F32 = jnp.float32
BF16 = jnp.bfloat16

M = 512
ROWS = 16
PAIRS = 3
OUTER, OWN, OTHER = 0, 1, 2
WAVES = 1
CW = M // WAVES
TILE = (8, 128)


def split(x):
    high = x.astype(BF16)
    return high, (x - high.astype(F32)).astype(BF16)


def total(x):
    return jnp.sum(jnp.sum(x, axis=0, keepdims=True), axis=1, keepdims=True)


def dot(a, b):
    return jnp.dot(a, b, preferred_element_type=F32)


def kernel(
    charges,
    coupling,
    w_in,
    pre_in,
    l_hbm,
    r_hbm,
    packed_out,
    raw,
    lcat,
    ltcat,
    rcat,
    rtcat,
    v,
    vcat,
    ycat,
    zcat,
    fbuf,
    tsum,
    otherbuf,
    bulk_half,
    bulk_full,
    tail3,
    tail7,
    tail2,
    image,
    corrected,
    held,
    arbuf,
    load_sem,
    z_s,
    z_r,
    ring_s,
    ring_r,
    other_s,
    other_r,
    rz_s,
    rz_r,
    rring_s,
    rring_r,
    rother_s,
    rother_r,
    ar_s,
    ar_r,
):
    zl, y, x = (lax.axis_index(a) for a in PAIR)
    zh, core = (lax.axis_index(a) for a in SECTOR)
    far = lax.rem(zh + 2 * core + 3, 4)
    places = (x, zl * 4 + y, zh * 2 + core)
    sizes = (4, 8, 8)
    away = [{"zl": q, "zh": far, "core": 1 - core} for q in range(2)]
    partner = {"core": 1 - core}
    in_x = [{"x": (x + d) & 3} for d in range(4)]
    in_y = [{"y": (y + d) & 3} for d in range(4)]
    in_yz = [{"zl": ((places[1] + d) & 7) >> 2, "y": (places[1] + d) & 3} for d in range(8)]
    in_sector = [{"zh": ((places[2] + d) & 7) >> 1, "core": (places[2] + d) & 1} for d in range(8)]

    def along_x(d):
        return in_x[d]

    def along_y(d):
        return in_y[d]

    def along_yz(d):
        return in_yz[d]

    def along_sector(d):
        return in_sector[d]

    peers = (along_x, along_yz, along_sector)

    def copy(src, dst, send, recv, device):
        return pltpu.make_async_remote_copy(
            src_ref=src,
            dst_ref=dst,
            send_sem=send,
            recv_sem=recv,
            device_id=device,
            device_id_type=MESH,
        )

    loads = []
    for p in range(PAIRS):
        loads.append(
            (
                pltpu.make_async_copy(l_hbm.at[p], raw.at[0, p], load_sem.at[0, p]),
                pltpu.make_async_copy(r_hbm.at[p], raw.at[1, p], load_sem.at[1, p]),
            )
        )
        for c in loads[-1]:
            c.start()

    barrier = pltpu.get_barrier_semaphore()
    signals = [g(d) for g, n in zip(peers, sizes) for d in range(1, n)]
    signals.append({"zl": 1 - zl, "zh": far, "core": 1 - core})
    for device in signals:
        pl.semaphore_signal(barrier, inc=1, device_id=device, device_id_type=MESH)

    roles, weights = [], []
    for p in range(PAIRS):
        charge = charges[p]
        roles.append(jnp.where(core == 0, charge, 2 - charge))
        weights.append(coupling[0, charge].astype(F32))

    def gathering(app):
        block = v.at[app]
        sends = []

        def begin(copies):
            for c in copies:
                c.start()
            sends.extend(copies)

        def wave_steps(wave):
            cols = pl.ds(wave * CW, CW)
            mine = block.at[OWN, zl, y, x, :, cols]

            def ring(phase, ref, group, n):
                return [
                    copy(
                        ref,
                        ref,
                        ring_s.at[app, wave, phase, d - 1],
                        ring_r.at[app, wave, phase, d - 1],
                        group(d),
                    )
                    for d in range(1, n)
                ]

            across = [
                copy(
                    mine,
                    block.at[OUTER, zl, y, x, :, cols],
                    z_s.at[app, wave, q],
                    z_r.at[app, wave, zl],
                    away[q],
                )
                for q in range(2)
            ]
            own1 = ring(0, mine, along_yz, 8)
            outer1 = ring(2, block.at[OUTER, :, y, x, :, cols], along_x, 4)

            def two_way(phase, unit, i, group):
                def one(ref, d, k):
                    return copy(
                        ref, ref, ring_s.at[app, wave, phase, k], ring_r.at[app, wave, phase, k], group(d)
                    )

                first = [
                    one(unit(i, 0), 1, 0),
                    one(unit(i, 1), 3, 1),
                    one(unit(i, 1), 1, 2),
                    one(unit(i, 0), 3, 3),
                ]
                onward = [
                    one(unit(lax.rem(i + 3, 4), 0), 1, 4),
                    one(unit(lax.rem(i + 1, 4), 1), 3, 5),
                ]
                return first, onward

            own2, own2_on = two_way(1, lambda i, h: block.at[OWN, h, :, i, :, cols], x, along_x)
            outer2, outer2_on = two_way(
                3, lambda i, h: block.at[OUTER, h, i, :, :, cols], y, along_y
            )
            onto = copy(
                block.at[OWN, :, :, :, :, cols],
                block.at[OTHER, :, :, :, :, cols],
                other_s.at[app, wave],
                other_r.at[app, wave],
                partner,
            )

            def arrived(copies):
                for c in copies:
                    c.wait_recv()

            def outer_first():
                for q in range(2):
                    there = block.at[OUTER, q, y, x, :, cols]
                    copy(
                        there, there, z_s.at[app, wave, q], z_r.at[app, wave, q], away[q]
                    ).wait_recv()
                begin(outer1)

            def own_second():
                arrived(own1)
                begin(own2)

            def outer_second():
                arrived(outer1)
                begin(outer2)

            def pass_on(first, onward):
                for k in range(2):
                    first[k].wait_recv()
                    begin([onward[k]])

            def hand_over():
                arrived(own2[2:] + own2_on)
                begin([onto])

            return {
                "across": lambda: begin(across),
                "own1": lambda: begin(own1),
                "outer1": outer_first,
                "own2": own_second,
                "outer2": outer_second,
                "own": hand_over,
                "own2_on": lambda: pass_on(own2, own2_on),
                "outer2_on": lambda: pass_on(outer2, outer2_on),
                "outer": lambda: arrived(outer2[2:] + outer2_on),
                "other": onto.wait_recv,
            }

        return [wave_steps(w) for w in range(WAVES)], sends

    def summing(app):
        sends = []

        def begin(copies):
            for c in copies:
                c.start()
            sends.extend(copies)

        def arrived(copies):
            for c in copies:
                c.wait_recv()

        def wave_steps(wave):
            cols = pl.ds(wave * CW, CW)

            def ring(phase, chunk, into, group, n):
                return [
                    copy(
                        chunk(d),
                        into.at[d - 1],
                        rring_s.at[app, wave, phase, d - 1],
                        rring_r.at[app, wave, phase, d - 1],
                        group(d),
                    )
                    for d in range(1, n)
                ]

            small_outer, small_own, crossed = tail3.at[wave], tail7.at[wave], tail2.at[app, wave]
            def two_way(phase, chunk, half, full, i, group):
                def one(src, dst, d, k):
                    return copy(
                        src, dst, rring_s.at[app, wave, phase, k], rring_r.at[app, wave, phase, k], group(d)
                    )

                right, left, opposite = lax.rem(i + 1, 4), lax.rem(i + 3, 4), lax.rem(i + 2, 4)
                first = [
                    one(chunk(opposite, 0), half.at[0], 1, 0),
                    one(chunk(opposite, 1), half.at[1], 3, 1),
                    one(chunk(right, 1), full.at[0, 1], 1, 2),
                    one(chunk(left, 0), full.at[1, 0], 3, 3),
                ]
                onward = [
                    one(chunk(right, 0), full.at[0, 0], 1, 4),
                    one(chunk(left, 1), full.at[1, 1], 3, 5),
                ]

                def pass_on():
                    for k, mine in enumerate((chunk(right, 0), chunk(left, 1))):
                        first[k].wait_recv()
                        mine[...] += half[k]
                        begin([onward[k]])

                def finish():
                    arrived(first[2:] + onward)
                    for h in range(2):
                        mine = chunk(i, h)
                        mine[...] += full[0, h] + full[1, h]

                return first, pass_on, finish

            outer2, outer2_on, outer2_end = two_way(
                0,
                lambda d, h: tsum.at[OUTER, h, d, :, :, cols],
                bulk_half.at[wave, 0],
                bulk_full.at[wave, 0],
                y,
                along_y,
            )
            own2, own2_on, own2_end = two_way(
                1,
                lambda d, h: tsum.at[OWN, h, :, d, :, cols],
                bulk_half.at[wave, 1],
                bulk_full.at[wave, 1],
                x,
                along_x,
            )
            outer1 = ring(
                2,
                lambda d: tsum.at[OUTER, :, y, lax.rem(x + d, 4), :, cols],
                small_outer,
                along_x,
                4,
            )

            def to_yz(d):
                place = lax.rem(places[1] + d, 8)
                return tsum.at[OWN, place // 4, lax.rem(place, 4), x, :, cols]

            own1 = ring(3, to_yz, small_own, along_yz, 8)
            across = [
                copy(
                    tsum.at[OUTER, q, y, x, :, cols],
                    crossed.at[zl],
                    rz_s.at[app, wave, q],
                    rz_r.at[app, wave, zl],
                    away[q],
                )
                for q in range(2)
            ]
            onto = copy(
                tsum.at[OTHER, :, :, :, :, cols],
                otherbuf.at[app, wave],
                rother_s.at[app, wave],
                rother_r.at[app, wave],
                partner,
            )

            def outer_first():
                outer2_end()
                begin(outer1)

            def own_first():
                own2_end()
                begin(own1)

            def outer_across():
                arrived(outer1)
                tsum[OUTER, :, y, x, :, cols] += small_outer[0] + (
                    small_outer[1] + small_outer[2]
                )
                begin(across)

            def own_done():
                arrived(own1)
                image[:, cols] = tsum[OWN, zl, y, x, :, cols] + jnp.sum(small_own[...], axis=0)

            def collect():
                for q in range(2):
                    copy(
                        tsum.at[OUTER, q, y, x, :, cols],
                        crossed.at[q],
                        rz_s.at[app, wave, q],
                        rz_r.at[app, wave, q],
                        away[q],
                    ).wait_recv()
                image[:, cols] += crossed[0] + crossed[1]

            return {
                "outer2": lambda: begin(outer2),
                "own2": lambda: begin(own2),
                "other": lambda: begin([onto]),
                "take": onto.wait_recv,
                "outer2_on": outer2_on,
                "own2_on": own2_on,
                "outer1": outer_first,
                "own1": own_first,
                "across": outer_across,
                "own": own_done,
                "collect": collect,
            }

        return [wave_steps(w) for w in range(WAVES)], sends

    class Reduction:
        def __init__(self, k, tile):
            self.k, self.stage = k, 0
            self.send(tile)

        def send(self, tile):
            stage, place = self.stage, places[self.stage]
            self.buf = arbuf.at[self.k, stage]
            self.buf[place] = tile
            mine = self.buf.at[place]
            for d in range(1, sizes[stage]):
                copy(
                    mine,
                    mine,
                    ar_s.at[self.k, stage],
                    ar_r.at[self.k, stage],
                    peers[stage](d),
                ).start()

        def step(self):
            stage, n = self.stage, sizes[self.stage]
            many = self.buf.at[pl.ds(0, n - 1)]
            waited = copy(
                many, many, ar_s.at[self.k, stage], ar_r.at[self.k, stage], peers[stage](1)
            )
            waited.wait_recv()
            waited.wait_send()
            tile = jnp.sum(self.buf[pl.ds(0, n)], axis=0)
            self.stage += 1
            if self.stage < 3:
                self.send(tile)
            return tile

    def packed(*values):
        row = lax.broadcasted_iota(jnp.int32, TILE, 0)
        tile = jnp.zeros(TILE, F32)
        for k, value in enumerate(values):
            tile = jnp.where(row == k, value, tile)
        return tile

    def prepare(p):
        for c in loads[p]:
            c.wait()

        @pl.loop(0, 4)
        def _(step):
            at = pl.multiple_of(step * 128, 128)
            at2 = pl.multiple_of(at + M, 128)
            at3 = pl.multiple_of(at + 2 * M, 128)
            rows = pl.ds(at, 128)
            left_rows, right_rows = raw[0, p, rows, :], raw[1, p, rows, :]
            hi, lo = split(left_rows)
            lcat[p, rows, 0:M] = hi
            lcat[p, rows, M : 2 * M] = hi
            lcat[p, rows, 2 * M :] = lo
            hi, lo = split(left_rows.T)
            ltcat[p, :, rows] = hi
            ltcat[p, :, pl.ds(at2, 128)] = hi
            ltcat[p, :, pl.ds(at3, 128)] = lo
            hi, lo = split(right_rows)
            rcat[p, rows, :] = hi
            rcat[p, pl.ds(at2, 128), :] = hi
            rcat[p, pl.ds(at3, 128), :] = lo
            hi, lo = split(right_rows.T)
            for third, part in enumerate((hi, hi, lo)):
                rtcat[p, third * M : (third + 1) * M, rows] = part

    def halve(app, role, wave):
        cols = pl.ds(wave * CW, CW)

        @pl.loop(0, 8)
        def _(step):
            h, j = step // 4, lax.rem(step, 4)
            at = pl.multiple_of(step * 64, 64)
            hi, lo = split(v[app, role, h, j, :, :, cols].reshape(64, CW))
            vcat[role, pl.ds(at, 64), cols] = hi
            vcat[role, pl.ds(pl.multiple_of(at + M, 64), 64), cols] = lo
            vcat[role, pl.ds(pl.multiple_of(at + 2 * M, 64), 64), cols] = hi

    def first_products(wave, forward):
        cols = pl.ds(wave * CW, CW)
        for p in range(PAIRS):
            if forward:
                hi, lo = split(dot(lcat[p], vcat[OWN, :, cols]))
                into = ycat
            else:
                hi, lo = split(weights[p] * dot(ltcat[p], vcat[roles[p], :, cols]))
                into = zcat
            for third, part in enumerate((hi, lo, hi)):
                into[p, :, third * M + wave * CW : third * M + (wave + 1) * CW] = part

    def forward_terms(app, wave):
        cols = pl.ds(wave * CW, CW)
        for p in range(PAIRS):
            fbuf[p] = dot(ycat[p], rtcat[p, :, cols])
        factors = [
            [jnp.where(roles[p] == r, weights[p], 0.0) for p in range(PAIRS)] for r in range(3)
        ]

        def body(step, acc):
            h, j = step // 4, lax.rem(step, 4)
            rows = pl.ds(pl.multiple_of(step * 64, 64), 64)
            f = [fbuf[p, rows, :] for p in range(PAIRS)]
            for r in range(3):
                term = factors[r][0] * f[0] + factors[r][1] * f[1] + factors[r][2] * f[2]
                tsum[r, h, j, :, :, cols] = term.reshape(4, ROWS, CW)
                both = term * v[app, r, h, j, :, :, cols].reshape(64, CW)
                acc = acc + jnp.sum(both.reshape(8, 8, CW), axis=0)
            return acc

        return lax.fori_loop(0, 8, body, jnp.zeros((8, CW), F32))

    def backward_terms(wave):
        cols = pl.ds(wave * CW, CW)
        for p in range(PAIRS):
            fbuf[p] = dot(zcat[p], rcat[p, :, cols])

    def join(app, wave):
        cols = pl.ds(wave * CW, CW)

        @pl.loop(0, 8)
        def _(step):
            h, j = step // 4, lax.rem(step, 4)
            rows = pl.ds(pl.multiple_of(step * 64, 64), 64)
            back = fbuf[0, rows, :] + fbuf[1, rows, :] + fbuf[2, rows, :]
            tsum[OWN, h, j, :, :, cols] += (
                back.reshape(4, ROWS, CW) + otherbuf[app, wave, h, j]
            )

    def apply(app, source, scalars, settle, then):
        v[app, OWN, zl, y, x] = source
        gather, gather_sends = gathering(app)
        summed, sum_sends = summing(app)
        for step in ("across", "own1"):
            for g in gather:
                g[step]()
        values = scalars()
        for p, step in enumerate(("outer1", "own2", "outer2")):
            if app == 0:
                prepare(p)
            for g in gather:
                g[step]()
        for g in gather:
            g["own2_on"]()
            g["outer2_on"]()
        for w, g in enumerate(gather):
            g["own"]()
            halve(app, OWN, w)
            first_products(w, True)
        for w, g in enumerate(gather):
            g["other"]()
            halve(app, OTHER, w)
            g["outer"]()
            halve(app, OUTER, w)
            first_products(w, False)
        part = jnp.zeros((8, CW), F32)
        for w, s in enumerate(summed):
            part += forward_terms(app, w)
            s["other"]()
            s["outer2"]()
            if w == WAVES - 1:
                full = Reduction(app, packed(2.0 * total(part), *values))
            backward_terms(w)
            s["take"]()
            join(app, w)
            s["own2"]()
            if w:
                summed[w - 1]["outer2_on"]()
                summed[w - 1]["own2_on"]()
        summed[-1]["outer2_on"]()
        summed[-1]["own2_on"]()
        full.step()
        for s in summed:
            s["outer1"]()
            s["own1"]()
        full.step()
        for s in summed:
            s["across"]()
        for s in summed:
            s["own"]()
        then(full.step())
        for s in summed:
            s["collect"]()
        for c in gather_sends + sum_sends:
            c.wait_send()
        return []

    pl.semaphore_wait(barrier, len(signals))
    w = w_in[...]
    known = {}

    def first_sums(sums):
        correlation, norm_sq = sums[0:1, 0:1], sums[1:2, 0:1]
        known["theta"] = correlation / norm_sq
        known["inverse"] = lax.rsqrt(norm_sq)

    sends = apply(0, w, lambda: (total(w * w),), lambda: None, first_sums)
    theta, inverse = known["theta"], known["inverse"]
    vector = w * inverse
    first = image[...] * inverse
    correction = (first - theta * vector) / pre_in[...]
    corrected[...] = correction
    held[...] = first

    def settle():
        for c in sends:
            c.wait_send()

    def second_sums(sums):
        product, along, squared, with_image = (sums[k : k + 1, 0:1] for k in range(4))
        length_sq = squared - along * along
        scale_back = lax.rsqrt(length_sq + 1e-30)
        corner = (
            scale_back * scale_back * (product - 2.0 * along * with_image + along * along * theta)
        )
        cross = scale_back * (with_image - along * theta)
        half = (theta - corner) / 2.0
        lowest = (theta + corner) / 2.0 - jnp.sqrt(half * half + cross * cross)
        u1 = corner - lowest
        u2 = -cross
        size_norm = jnp.sqrt(u1 * u1 + u2 * u2 + 1e-30)
        scale = math.sqrt(8 * M * M)
        one, two = scale * u1 / size_norm, scale * u2 / size_norm
        vector, first = w_in[...] * inverse, held[...]
        basis = (corrected[...] - along * vector) * scale_back
        packed_out[0:ROWS, :] = one * vector + two * basis
        lane = lax.broadcasted_iota(jnp.int32, TILE, 1)
        packed_out[2 * ROWS :, 0:128] = jnp.where(lane == 0, theta, lowest)
        known["rest"] = one, two * scale_back, along

    last_sends = apply(
        1,
        correction,
        lambda: (
            total(vector * correction),
            total(correction * correction),
            total(first * correction),
        ),
        settle,
        second_sums,
    )
    one, two, along = known["rest"]
    first = held[...]
    packed_out[ROWS : 2 * ROWS, :] = one * first + two * (image[...] - along * first)
    for c in last_sends:
        c.wait_send()


def per_device(wavefunction, preconditioner, left_ops, right_ops, charges, coupling):
    vmem = pl.BlockSpec(memory_space=pltpu.VMEM)
    smem = pl.BlockSpec(memory_space=pltpu.SMEM)
    dma = pltpu.SemaphoreType.DMA
    out = pl.pallas_call(
        kernel,
        out_shape=jax.ShapeDtypeStruct((2 * ROWS + 8, M), F32),
        in_specs=[smem, smem, vmem, vmem]
        + [pl.BlockSpec(memory_space=pl.ANY)] * 2,
        out_specs=vmem,
        scratch_shapes=[
            pltpu.VMEM((2, PAIRS, M, M), F32),
            pltpu.VMEM((PAIRS, M, 3 * M), BF16),
            pltpu.VMEM((PAIRS, M, 3 * M), BF16),
            pltpu.VMEM((PAIRS, 3 * M, M), BF16),
            pltpu.VMEM((PAIRS, 3 * M, M), BF16),
            pltpu.VMEM((2, 3, 2, 4, 4, ROWS, M), F32),
            pltpu.VMEM((3, 3 * M, M), BF16),
            pltpu.VMEM((PAIRS, M, 3 * M), BF16),
            pltpu.VMEM((PAIRS, M, 3 * M), BF16),
            pltpu.VMEM((PAIRS, M, CW), F32),
            pltpu.VMEM((3, 2, 4, 4, ROWS, M), F32),
            pltpu.VMEM((2, WAVES, 2, 4, 4, ROWS, CW), F32),
            pltpu.VMEM((WAVES, 2, 2, 4, ROWS, CW), F32),
            pltpu.VMEM((WAVES, 2, 2, 2, 4, ROWS, CW), F32),
            pltpu.VMEM((WAVES, 3, 2, ROWS, CW), F32),
            pltpu.VMEM((WAVES, 7, ROWS, CW), F32),
            pltpu.VMEM((2, WAVES, 2, ROWS, CW), F32),
            pltpu.VMEM((ROWS, M), F32),
            pltpu.VMEM((ROWS, M), F32),
            pltpu.VMEM((ROWS, M), F32),
            pltpu.VMEM((2, 3, 8) + TILE, F32),
            dma((2, PAIRS)),
            dma((2, WAVES, 2)),
            dma((2, WAVES, 2)),
            dma((2, WAVES, 4, 7)),
            dma((2, WAVES, 4, 7)),
            dma((2, WAVES,)),
            dma((2, WAVES,)),
            dma((2, WAVES, 2)),
            dma((2, WAVES, 2)),
            dma((2, WAVES, 4, 7)),
            dma((2, WAVES, 4, 7)),
            dma((2, WAVES,)),
            dma((2, WAVES,)),
            dma((2, 3)),
            dma((2, 3)),
        ],
        compiler_params=pltpu.CompilerParams(
            collective_id=0, has_side_effects=True, vmem_limit_bytes=60 * 1024 * 1024
        ),
    )(
        charges,
        coupling,
        wavefunction.reshape(ROWS, M),
        preconditioner.reshape(ROWS, M),
        left_ops.reshape(PAIRS, M, M),
        right_ops.reshape(PAIRS, M, M),
    )
    return out[None, 0:ROWS], out[None, ROWS : 2 * ROWS], out[2 * ROWS, 0:2]


def solution(mesh):
    split_mesh = Mesh(mesh.devices.reshape(2, 4, 4, 4, 2), PAIR + SECTOR)
    placed = (
        P(SECTOR, PAIR, None),
        P(SECTOR, PAIR, None),
        P(PAIR, SECTOR, None, None),
        P(PAIR, SECTOR, None, None),
        P(PAIR),
        P(SECTOR, None),
    )
    return jax.shard_map(
        per_device,
        mesh=split_mesh,
        in_specs=placed,
        out_specs=(P(SECTOR, PAIR, None), P(SECTOR, PAIR, None), P()),
        check_vma=False,
    )
```

```python
import math

import jax
import jax.numpy as jnp
from jax import lax
from jax.experimental import pallas as pl
from jax.experimental.pallas import tpu as pltpu
from jax.sharding import Mesh
from jax.sharding import PartitionSpec as P

SECTOR = ("zh", "core")
PAIR = ("zl", "y", "x")
MESH = pl.DeviceIdType.MESH
F32 = jnp.float32
BF16 = jnp.bfloat16

M = 512
ROWS = 16
PAIRS = 3
OUTER, OWN, OTHER = 0, 1, 2
WAVES = 1
CW = M // WAVES
TILE = (8, 128)


def split(x):
    high = x.astype(BF16)
    return high, (x - high.astype(F32)).astype(BF16)


def total(x):
    return jnp.sum(jnp.sum(x, axis=0, keepdims=True), axis=1, keepdims=True)


def dot(a, b):
    return jnp.dot(a, b, preferred_element_type=F32)


def kernel(
    charges,
    coupling,
    w_in,
    pre_in,
    l_hbm,
    r_hbm,
    packed_out,
    raw,
    lcat,
    ltcat,
    rcat,
    rtcat,
    v,
    vcat,
    ycat,
    zcat,
    fbuf,
    tsum,
    otherbuf,
    bulk_half,
    bulk_full,
    tail3,
    tail7,
    tail2,
    image,
    corrected,
    held,
    arbuf,
    load_sem,
    z_s,
    z_r,
    ring_s,
    ring_r,
    other_s,
    other_r,
    rz_s,
    rz_r,
    rring_s,
    rring_r,
    rother_s,
    rother_r,
    ar_s,
    ar_r,
):
    zl, y, x = (lax.axis_index(a) for a in PAIR)
    zh, core = (lax.axis_index(a) for a in SECTOR)
    far = lax.rem(zh + 2 * core + 3, 4)
    places = (x, zl * 4 + y, zh * 2 + core)
    sizes = (4, 8, 8)
    away = [{"zl": q, "zh": far, "core": 1 - core} for q in range(2)]
    partner = {"core": 1 - core}
    in_x = [{"x": (x + d) & 3} for d in range(4)]
    in_y = [{"y": (y + d) & 3} for d in range(4)]
    in_yz = [{"zl": ((places[1] + d) & 7) >> 2, "y": (places[1] + d) & 3} for d in range(8)]
    in_sector = [{"zh": ((places[2] + d) & 7) >> 1, "core": (places[2] + d) & 1} for d in range(8)]

    def along_x(d):
        return in_x[d]

    def along_y(d):
        return in_y[d]

    def along_yz(d):
        return in_yz[d]

    def along_sector(d):
        return in_sector[d]

    peers = (along_x, along_yz, along_sector)

    def copy(src, dst, send, recv, device):
        return pltpu.make_async_remote_copy(
            src_ref=src,
            dst_ref=dst,
            send_sem=send,
            recv_sem=recv,
            device_id=device,
            device_id_type=MESH,
        )

    loads = []
    for p in range(PAIRS):
        loads.append(
            (
                pltpu.make_async_copy(l_hbm.at[p], raw.at[0, p], load_sem.at[0, p]),
                pltpu.make_async_copy(r_hbm.at[p], raw.at[1, p], load_sem.at[1, p]),
            )
        )
        for c in loads[-1]:
            c.start()

    barrier = pltpu.get_barrier_semaphore()
    signals = [g(d) for g, n in zip(peers, sizes) for d in range(1, n)]
    signals.append({"zl": 1 - zl, "zh": far, "core": 1 - core})
    for device in signals:
        pl.semaphore_signal(barrier, inc=1, device_id=device, device_id_type=MESH)

    roles, weights = [], []
    for p in range(PAIRS):
        charge = charges[p]
        roles.append(jnp.where(core == 0, charge, 2 - charge))
        weights.append(coupling[0, charge].astype(F32))

    def gathering(app):
        block = v.at[app]
        sends = []

        def begin(copies):
            for c in copies:
                c.start()
            sends.extend(copies)

        def wave_steps(wave):
            cols = pl.ds(wave * CW, CW)
            mine = block.at[OWN, zl, y, x, :, cols]

            def ring(phase, ref, group, n):
                return [
                    copy(
                        ref,
                        ref,
                        ring_s.at[app, wave, phase, d - 1],
                        ring_r.at[app, wave, phase, d - 1],
                        group(d),
                    )
                    for d in range(1, n)
                ]

            across = [
                copy(
                    mine,
                    block.at[OUTER, zl, y, x, :, cols],
                    z_s.at[app, wave, q],
                    z_r.at[app, wave, zl],
                    away[q],
                )
                for q in range(2)
            ]
            own1 = ring(0, mine, along_yz, 8)
            outer1 = ring(2, block.at[OUTER, :, y, x, :, cols], along_x, 4)

            def two_way(phase, unit, i, group):
                def one(ref, d, k):
                    return copy(
                        ref, ref, ring_s.at[app, wave, phase, k], ring_r.at[app, wave, phase, k], group(d)
                    )

                first = [
                    one(unit(i, 0), 1, 0),
                    one(unit(i, 1), 3, 1),
                    one(unit(i, 1), 1, 2),
                    one(unit(i, 0), 3, 3),
                ]
                onward = [
                    one(unit(lax.rem(i + 3, 4), 0), 1, 4),
                    one(unit(lax.rem(i + 1, 4), 1), 3, 5),
                ]
                return first, onward

            own2, own2_on = two_way(1, lambda i, h: block.at[OWN, h, :, i, :, cols], x, along_x)
            outer2, outer2_on = two_way(
                3, lambda i, h: block.at[OUTER, h, i, :, :, cols], y, along_y
            )
            onto = copy(
                block.at[OWN, :, :, :, :, cols],
                block.at[OTHER, :, :, :, :, cols],
                other_s.at[app, wave],
                other_r.at[app, wave],
                partner,
            )

            def arrived(copies):
                for c in copies:
                    c.wait_recv()

            def outer_first():
                for q in range(2):
                    there = block.at[OUTER, q, y, x, :, cols]
                    copy(
                        there, there, z_s.at[app, wave, q], z_r.at[app, wave, q], away[q]
                    ).wait_recv()
                begin(outer1)

            def own_second():
                arrived(own1)
                begin(own2)

            def outer_second():
                arrived(outer1)
                begin(outer2)

            def pass_on(first, onward):
                for k in range(2):
                    first[k].wait_recv()
                    begin([onward[k]])

            def hand_over():
                arrived(own2[2:] + own2_on)
                begin([onto])

            return {
                "across": lambda: begin(across),
                "own1": lambda: begin(own1),
                "outer1": outer_first,
                "own2": own_second,
                "outer2": outer_second,
                "own": hand_over,
                "own2_on": lambda: pass_on(own2, own2_on),
                "outer2_on": lambda: pass_on(outer2, outer2_on),
                "outer": lambda: arrived(outer2[2:] + outer2_on),
                "other": onto.wait_recv,
            }

        return [wave_steps(w) for w in range(WAVES)], sends

    def summing(app):
        sends = []

        def begin(copies):
            for c in copies:
                c.start()
            sends.extend(copies)

        def arrived(copies):
            for c in copies:
                c.wait_recv()

        def wave_steps(wave):
            cols = pl.ds(wave * CW, CW)

            def ring(phase, chunk, into, group, n):
                return [
                    copy(
                        chunk(d),
                        into.at[d - 1],
                        rring_s.at[app, wave, phase, d - 1],
                        rring_r.at[app, wave, phase, d - 1],
                        group(d),
                    )
                    for d in range(1, n)
                ]

            small_outer, small_own, crossed = tail3.at[wave], tail7.at[wave], tail2.at[app, wave]
            def two_way(phase, chunk, half, full, i, group):
                def one(src, dst, d, k):
                    return copy(
                        src, dst, rring_s.at[app, wave, phase, k], rring_r.at[app, wave, phase, k], group(d)
                    )

                right, left, opposite = lax.rem(i + 1, 4), lax.rem(i + 3, 4), lax.rem(i + 2, 4)
                first = [
                    one(chunk(opposite, 0), half.at[0], 1, 0),
                    one(chunk(opposite, 1), half.at[1], 3, 1),
                    one(chunk(right, 1), full.at[0, 1], 1, 2),
                    one(chunk(left, 0), full.at[1, 0], 3, 3),
                ]
                onward = [
                    one(chunk(right, 0), full.at[0, 0], 1, 4),
                    one(chunk(left, 1), full.at[1, 1], 3, 5),
                ]

                def pass_on():
                    for k, mine in enumerate((chunk(right, 0), chunk(left, 1))):
                        first[k].wait_recv()
                        mine[...] += half[k]
                        begin([onward[k]])

                def finish():
                    arrived(first[2:] + onward)
                    for h in range(2):
                        mine = chunk(i, h)
                        mine[...] += full[0, h] + full[1, h]

                return first, pass_on, finish

            outer2, outer2_on, outer2_end = two_way(
                0,
                lambda d, h: tsum.at[OUTER, h, d, :, :, cols],
                bulk_half.at[wave, 0],
                bulk_full.at[wave, 0],
                y,
                along_y,
            )
            own2, own2_on, own2_end = two_way(
                1,
                lambda d, h: tsum.at[OWN, h, :, d, :, cols],
                bulk_half.at[wave, 1],
                bulk_full.at[wave, 1],
                x,
                along_x,
            )
            outer1 = ring(
                2,
                lambda d: tsum.at[OUTER, :, y, lax.rem(x + d, 4), :, cols],
                small_outer,
                along_x,
                4,
            )

            def to_yz(d):
                place = lax.rem(places[1] + d, 8)
                return tsum.at[OWN, place // 4, lax.rem(place, 4), x, :, cols]

            own1 = ring(3, to_yz, small_own, along_yz, 8)
            across = [
                copy(
                    tsum.at[OUTER, q, y, x, :, cols],
                    crossed.at[zl],
                    rz_s.at[app, wave, q],
                    rz_r.at[app, wave, zl],
                    away[q],
                )
                for q in range(2)
            ]
            onto = copy(
                tsum.at[OTHER, :, :, :, :, cols],
                otherbuf.at[app, wave],
                rother_s.at[app, wave],
                rother_r.at[app, wave],
                partner,
            )

            def outer_first():
                outer2_end()
                begin(outer1)

            def own_first():
                own2_end()
                begin(own1)

            def outer_across():
                arrived(outer1)
                tsum[OUTER, :, y, x, :, cols] += small_outer[0] + (
                    small_outer[1] + small_outer[2]
                )
                begin(across)

            def own_done():
                arrived(own1)
                image[:, cols] = tsum[OWN, zl, y, x, :, cols] + jnp.sum(small_own[...], axis=0)

            def collect():
                for q in range(2):
                    copy(
                        tsum.at[OUTER, q, y, x, :, cols],
                        crossed.at[q],
                        rz_s.at[app, wave, q],
                        rz_r.at[app, wave, q],
                        away[q],
                    ).wait_recv()
                image[:, cols] += crossed[0] + crossed[1]

            return {
                "outer2": lambda: begin(outer2),
                "own2": lambda: begin(own2),
                "other": lambda: begin([onto]),
                "take": onto.wait_recv,
                "outer2_on": outer2_on,
                "own2_on": own2_on,
                "outer1": outer_first,
                "own1": own_first,
                "across": outer_across,
                "own": own_done,
                "collect": collect,
            }

        return [wave_steps(w) for w in range(WAVES)], sends

    class Reduction:
        def __init__(self, k, tile):
            self.k, self.stage = k, 0
            self.send(tile)

        def send(self, tile):
            stage, place = self.stage, places[self.stage]
            self.buf = arbuf.at[self.k, stage]
            self.buf[place] = tile
            mine = self.buf.at[place]
            for d in range(1, sizes[stage]):
                copy(
                    mine,
                    mine,
                    ar_s.at[self.k, stage],
                    ar_r.at[self.k, stage],
                    peers[stage](d),
                ).start()

        def step(self):
            stage, n = self.stage, sizes[self.stage]
            many = self.buf.at[pl.ds(0, n - 1)]
            waited = copy(
                many, many, ar_s.at[self.k, stage], ar_r.at[self.k, stage], peers[stage](1)
            )
            waited.wait_recv()
            waited.wait_send()
            tile = jnp.sum(self.buf[pl.ds(0, n)], axis=0)
            self.stage += 1
            if self.stage < 3:
                self.send(tile)
            return tile

    def packed(*values):
        row = lax.broadcasted_iota(jnp.int32, TILE, 0)
        tile = jnp.zeros(TILE, F32)
        for k, value in enumerate(values):
            tile = jnp.where(row == k, value, tile)
        return tile

    def prepare(p):
        for c in loads[p]:
            c.wait()

        @pl.loop(0, 4)
        def _(step):
            at = pl.multiple_of(step * 128, 128)
            at2 = pl.multiple_of(at + M, 128)
            at3 = pl.multiple_of(at + 2 * M, 128)
            rows = pl.ds(at, 128)
            left_rows, right_rows = raw[0, p, rows, :], raw[1, p, rows, :]
            hi, lo = split(left_rows)
            lcat[p, rows, 0:M] = hi
            lcat[p, rows, M : 2 * M] = hi
            lcat[p, rows, 2 * M :] = lo
            hi, lo = split(left_rows.T)
            ltcat[p, :, rows] = hi
            ltcat[p, :, pl.ds(at2, 128)] = hi
            ltcat[p, :, pl.ds(at3, 128)] = lo
            hi, lo = split(right_rows)
            rcat[p, rows, :] = hi
            rcat[p, pl.ds(at2, 128), :] = hi
            rcat[p, pl.ds(at3, 128), :] = lo
            hi, lo = split(right_rows.T)
            for third, part in enumerate((hi, hi, lo)):
                rtcat[p, third * M : (third + 1) * M, rows] = part

    def halve(app, role, wave):
        cols = pl.ds(wave * CW, CW)

        @pl.loop(0, 8)
        def _(step):
            h, j = step // 4, lax.rem(step, 4)
            at = pl.multiple_of(step * 64, 64)
            hi, lo = split(v[app, role, h, j, :, :, cols].reshape(64, CW))
            vcat[role, pl.ds(at, 64), cols] = hi
            vcat[role, pl.ds(pl.multiple_of(at + M, 64), 64), cols] = lo
            vcat[role, pl.ds(pl.multiple_of(at + 2 * M, 64), 64), cols] = hi

    def first_products(wave, forward):
        cols = pl.ds(wave * CW, CW)
        for p in range(PAIRS):
            if forward:
                hi, lo = split(dot(lcat[p], vcat[OWN, :, cols]))
                into = ycat
            else:
                hi, lo = split(weights[p] * dot(ltcat[p], vcat[roles[p], :, cols]))
                into = zcat
            for third, part in enumerate((hi, lo, hi)):
                into[p, :, third * M + wave * CW : third * M + (wave + 1) * CW] = part

    def forward_terms(app, wave):
        cols = pl.ds(wave * CW, CW)
        for p in range(PAIRS):
            fbuf[p] = dot(ycat[p], rtcat[p, :, cols])
        factors = [
            [jnp.where(roles[p] == r, weights[p], 0.0) for p in range(PAIRS)] for r in range(3)
        ]

        def body(step, acc):
            h, j = step // 4, lax.rem(step, 4)
            rows = pl.ds(pl.multiple_of(step * 64, 64), 64)
            f = [fbuf[p, rows, :] for p in range(PAIRS)]
            for r in range(3):
                term = factors[r][0] * f[0] + factors[r][1] * f[1] + factors[r][2] * f[2]
                tsum[r, h, j, :, :, cols] = term.reshape(4, ROWS, CW)
                both = term * v[app, r, h, j, :, :, cols].reshape(64, CW)
                acc = acc + jnp.sum(both.reshape(8, 8, CW), axis=0)
            return acc

        return lax.fori_loop(0, 8, body, jnp.zeros((8, CW), F32))

    def backward_terms(wave):
        cols = pl.ds(wave * CW, CW)
        for p in range(PAIRS):
            fbuf[p] = dot(zcat[p], rcat[p, :, cols])

    def join(app, wave):
        cols = pl.ds(wave * CW, CW)

        @pl.loop(0, 8)
        def _(step):
            h, j = step // 4, lax.rem(step, 4)
            rows = pl.ds(pl.multiple_of(step * 64, 64), 64)
            back = fbuf[0, rows, :] + fbuf[1, rows, :] + fbuf[2, rows, :]
            tsum[OWN, h, j, :, :, cols] += (
                back.reshape(4, ROWS, CW) + otherbuf[app, wave, h, j]
            )

    def apply(app, source, scalars, settle, then):
        v[app, OWN, zl, y, x] = source
        gather, gather_sends = gathering(app)
        summed, sum_sends = summing(app)
        for step in ("across", "own1"):
            for g in gather:
                g[step]()
        values = scalars()
        for p, step in enumerate(("outer1", "own2", "outer2")):
            if app == 0:
                prepare(p)
            for g in gather:
                g[step]()
        for g in gather:
            g["own2_on"]()
            g["outer2_on"]()
        for w, g in enumerate(gather):
            g["own"]()
            halve(app, OWN, w)
            first_products(w, True)
        for w, g in enumerate(gather):
            g["other"]()
            halve(app, OTHER, w)
            g["outer"]()
            halve(app, OUTER, w)
            first_products(w, False)
        part = jnp.zeros((8, CW), F32)
        for w, s in enumerate(summed):
            part += forward_terms(app, w)
            s["other"]()
            s["outer2"]()
            backward_terms(w)
            s["take"]()
            join(app, w)
            s["own2"]()
            if w == WAVES - 1:
                full = Reduction(app, packed(2.0 * total(part), *values))
            if w:
                summed[w - 1]["outer2_on"]()
                summed[w - 1]["own2_on"]()
        summed[-1]["outer2_on"]()
        summed[-1]["own2_on"]()
        full.step()
        for s in summed:
            s["outer1"]()
            s["own1"]()
        full.step()
        for s in summed:
            s["across"]()
        for c in gather_sends:
            c.wait_send()
        for s in summed:
            s["own"]()
        then(full.step())
        for s in summed:
            s["collect"]()
        for c in sum_sends:
            c.wait_send()
        return []

    pl.semaphore_wait(barrier, len(signals))
    w = w_in[...]
    known = {}

    def first_sums(sums):
        correlation, norm_sq = sums[0:1, 0:1], sums[1:2, 0:1]
        known["theta"] = correlation / norm_sq
        known["inverse"] = lax.rsqrt(norm_sq)

    sends = apply(0, w, lambda: (total(w * w),), lambda: None, first_sums)
    theta, inverse = known["theta"], known["inverse"]
    vector = w * inverse
    first = image[...] * inverse
    correction = (first - theta * vector) / pre_in[...]
    corrected[...] = correction
    held[...] = first

    def settle():
        for c in sends:
            c.wait_send()

    def second_sums(sums):
        product, along, squared, with_image = (sums[k : k + 1, 0:1] for k in range(4))
        length_sq = squared - along * along
        scale_back = lax.rsqrt(length_sq + 1e-30)
        corner = (
            scale_back * scale_back * (product - 2.0 * along * with_image + along * along * theta)
        )
        cross = scale_back * (with_image - along * theta)
        half = (theta - corner) / 2.0
        lowest = (theta + corner) / 2.0 - jnp.sqrt(half * half + cross * cross)
        u1 = corner - lowest
        u2 = -cross
        size_norm = jnp.sqrt(u1 * u1 + u2 * u2 + 1e-30)
        scale = math.sqrt(8 * M * M)
        one, two = scale * u1 / size_norm, scale * u2 / size_norm
        vector, first = w_in[...] * inverse, held[...]
        basis = (corrected[...] - along * vector) * scale_back
        packed_out[0:ROWS, :] = one * vector + two * basis
        lane = lax.broadcasted_iota(jnp.int32, TILE, 1)
        packed_out[2 * ROWS :, 0:128] = jnp.where(lane == 0, theta, lowest)
        known["rest"] = one, two * scale_back, along

    last_sends = apply(
        1,
        correction,
        lambda: (
            total(vector * correction),
            total(correction * correction),
            total(first * correction),
        ),
        settle,
        second_sums,
    )
    one, two, along = known["rest"]
    first = held[...]
    packed_out[ROWS : 2 * ROWS, :] = one * first + two * (image[...] - along * first)
    for c in last_sends:
        c.wait_send()


def per_device(wavefunction, preconditioner, left_ops, right_ops, charges, coupling):
    vmem = pl.BlockSpec(memory_space=pltpu.VMEM)
    smem = pl.BlockSpec(memory_space=pltpu.SMEM)
    dma = pltpu.SemaphoreType.DMA
    out = pl.pallas_call(
        kernel,
        out_shape=jax.ShapeDtypeStruct((2 * ROWS + 8, M), F32),
        in_specs=[smem, smem, vmem, vmem]
        + [pl.BlockSpec(memory_space=pl.ANY)] * 2,
        out_specs=vmem,
        scratch_shapes=[
            pltpu.VMEM((2, PAIRS, M, M), F32),
            pltpu.VMEM((PAIRS, M, 3 * M), BF16),
            pltpu.VMEM((PAIRS, M, 3 * M), BF16),
            pltpu.VMEM((PAIRS, 3 * M, M), BF16),
            pltpu.VMEM((PAIRS, 3 * M, M), BF16),
            pltpu.VMEM((2, 3, 2, 4, 4, ROWS, M), F32),
            pltpu.VMEM((3, 3 * M, M), BF16),
            pltpu.VMEM((PAIRS, M, 3 * M), BF16),
            pltpu.VMEM((PAIRS, M, 3 * M), BF16),
            pltpu.VMEM((PAIRS, M, CW), F32),
            pltpu.VMEM((3, 2, 4, 4, ROWS, M), F32),
            pltpu.VMEM((2, WAVES, 2, 4, 4, ROWS, CW), F32),
            pltpu.VMEM((WAVES, 2, 2, 4, ROWS, CW), F32),
            pltpu.VMEM((WAVES, 2, 2, 2, 4, ROWS, CW), F32),
            pltpu.VMEM((WAVES, 3, 2, ROWS, CW), F32),
            pltpu.VMEM((WAVES, 7, ROWS, CW), F32),
            pltpu.VMEM((2, WAVES, 2, ROWS, CW), F32),
            pltpu.VMEM((ROWS, M), F32),
            pltpu.VMEM((ROWS, M), F32),
            pltpu.VMEM((ROWS, M), F32),
            pltpu.VMEM((2, 3, 8) + TILE, F32),
            dma((2, PAIRS)),
            dma((2, WAVES, 2)),
            dma((2, WAVES, 2)),
            dma((2, WAVES, 4, 7)),
            dma((2, WAVES, 4, 7)),
            dma((2, WAVES,)),
            dma((2, WAVES,)),
            dma((2, WAVES, 2)),
            dma((2, WAVES, 2)),
            dma((2, WAVES, 4, 7)),
            dma((2, WAVES, 4, 7)),
            dma((2, WAVES,)),
            dma((2, WAVES,)),
            dma((2, 3)),
            dma((2, 3)),
        ],
        compiler_params=pltpu.CompilerParams(
            collective_id=0, has_side_effects=True, vmem_limit_bytes=60 * 1024 * 1024
        ),
    )(
        charges,
        coupling,
        wavefunction.reshape(ROWS, M),
        preconditioner.reshape(ROWS, M),
        left_ops.reshape(PAIRS, M, M),
        right_ops.reshape(PAIRS, M, M),
    )
    return out[None, 0:ROWS], out[None, ROWS : 2 * ROWS], out[2 * ROWS, 0:2]


def solution(mesh):
    split_mesh = Mesh(mesh.devices.reshape(2, 4, 4, 4, 2), PAIR + SECTOR)
    placed = (
        P(SECTOR, PAIR, None),
        P(SECTOR, PAIR, None),
        P(PAIR, SECTOR, None, None),
        P(PAIR, SECTOR, None, None),
        P(PAIR),
        P(SECTOR, None),
    )
    return jax.shard_map(
        per_device,
        mesh=split_mesh,
        in_specs=placed,
        out_specs=(P(SECTOR, PAIR, None), P(SECTOR, PAIR, None), P()),
        check_vma=False,
    )
```
